32 devices in a mesh: wide: 16 (over z, y, x), narrow: 2 (over core).
Axes of the slice: x: 2, y: 2, z: 4, core: 2. Of those that a mesh axis runs over, the one named last changes fastest.
Arguments:
- grads: bfloat16 [14, 512, 2048], P(None, 'wide', 'narrow'), may hold values from -200 to 200
- momentum: float32 [14, 512, 2048], P(None, 'wide', 'narrow'), may hold values from -400 to 400
- owners: int32 [14], replicated, may hold values from 0 to 15, as said below
- norm_grads: float32 [28, 2048], P('narrow', 'wide'), may hold values from -6 to 6
- norm_params: float32 [28, 2048], P('narrow', 'wide'), may hold values from 0.5 to 1.5
- adam_m: float32 [28, 2048], P('narrow', 'wide'), may hold values from -4 to 4
- adam_v: float32 [28, 2048], P('narrow', 'wide'), may hold values from 0.1 to 4
Outputs:
- muon_update: bfloat16 [14, 512, 2048], P(None, 'wide', 'narrow')
- momentum_new: float32 [14, 512, 2048], P(None, 'wide', 'narrow')
- owner_load: float32 [16], P('wide')
- norm_params_new: float32 [28, 2048], P('narrow', 'wide')
- adam_m_new: float32 [28, 2048], P('narrow', 'wide')
- adam_v_new: float32 [28, 2048], P('narrow', 'wide')
The draws below stay inside these ranges and needn't reach their ends.
Inputs may be any that keep to these rules, and one draw needn't show every extreme that they name: `owners`: each of the 16 groups owns at most 2 matrices, and some group owns exactly 2.
All inputs are finite; a program needn't handle non-finite values.
Results may differ from the reference program's by a relative error of at most 0.014.
Values may be sent and summed in bfloat16 or wider, within the bound.
A program may use at most 64 MiB of HBM per device.

```python
import math
import jax
import jax.numpy as jnp
from jax import lax

D = 2048
KV_OUT = 512
ITERS = 2
CAP = 2
GROUPS = 16
MATS = 14
NVEC = 28
N_NARROW = 2


def field_draw(key, salt):
    key = jax.random.fold_in(key, salt)
    key_base, key_rows, key_cols = jax.random.split(key, 3)
    shape = (MATS, KV_OUT, D)
    row_place = jnp.arange(KV_OUT, dtype=jnp.float32) / KV_OUT
    col_place = jnp.arange(D, dtype=jnp.float32) / D
    row_scale = jnp.exp(jax.random.uniform(key_rows, (MATS, KV_OUT, 1), minval=0.0, maxval=2.3026))
    col_scale = jnp.exp(jax.random.uniform(key_cols, (MATS, 1, D), minval=0.0, maxval=2.3026))
    base = jnp.clip(jax.random.normal(key_base, shape), -5.0, 5.0)
    trend = (1.0 + 0.8 * row_place)[None, :, None] * (1.0 + 0.8 * col_place)[None, None, :]
    factor = 0.05
    return base * row_scale * col_scale * trend * factor


def draw_grads(key, part):
    return field_draw(key, 11).astype(jnp.bfloat16)


def draw_momentum(key, part):
    return (2.0 * field_draw(key, 23)).astype(jnp.float32)


def draw_owners(key, part):
    key = jax.random.fold_in(key, 37)
    slot_total = GROUPS * CAP
    places = jnp.arange(slot_total, dtype=jnp.int32)
    order = jax.random.permutation(key, slot_total).astype(jnp.int32)
    first_group = order[0] // CAP
    for member in range(1, CAP):
        target = first_group * CAP + (order[0] % CAP + member) % CAP
        where_target = jnp.argmax((order == target).astype(jnp.int32)).astype(jnp.int32)
        displaced = order[member]
        order = jnp.where(places == where_target, displaced, order)
        order = jnp.where(places == member, target, order)
    return (order[:MATS] // CAP).astype(jnp.int32)


def levels(own_key, dims, cuts, smallest, high):
    loudness, own = 1.0, jax.random.fold_in(own_key, 6)
    for position, shards_of in cuts:
        draws = jnp.exp(jax.random.uniform(jax.random.fold_in(own, position), (shards_of,), jnp.float32, smallest / len(cuts), high / len(cuts)))
        loudness = loudness * jnp.repeat(draws, dims[position] // shards_of).reshape([-1 if axis == position else 1 for axis in range(len(dims))])
    return loudness


def scatter_about(key, shape, spread, limit, shards=(), held_as=jnp.bfloat16):
    factor_of = levels(key, shape, shards, -0.22, 0.18) if shards else 1.0
    values = jax.random.normal(key, shape, jnp.float32) * spread * factor_of
    return jnp.minimum(jnp.maximum(values, -limit), limit).astype(held_as)


def setup_inputs(seed: int = 0) -> dict:
    keys = jax.random.split(jax.random.key(seed), 8)
    return {
        "grads": draw_grads(jax.random.fold_in(keys[7], 71), 0),
        "momentum": draw_momentum(jax.random.fold_in(keys[7], 71), 0),
        "owners": draw_owners(jax.random.fold_in(keys[7], 71), 0),
        "norm_grads": scatter_about(keys[3], (NVEC, D), 1.0, 6.0, ((0, 2), (1, 16)), jnp.float32),
        "norm_params": jnp.clip(1.0 + 0.1 * jax.random.normal(keys[4], (NVEC, D), jnp.float32), 0.5, 1.5),
        "adam_m": scatter_about(keys[5], (NVEC, D), 0.3, 4.0, ((0, 2), (1, 16)), jnp.float32),
        "adam_v": jnp.clip(jnp.exp(math.log(4.0) - 3.6888794 * jax.random.uniform(keys[6], (NVEC, D), jnp.float32) ** levels(keys[6], (NVEC, D), ((0, 2), (1, 16)), -0.2, 0.2)), 0.1, 4.0),
    }


coef_a = 3.4445
coef_b = -4.775
coef_c = 2.0315
muon_beta = 0.95
norm_eps = 1e-07
adam_first = 0.9
adam_second = 0.95
adam_rate = 0.02
adam_eps = 1e-08
first_fix = 1.0 - 0.9 ** 10
second_fix = 1.0 - 0.95 ** 10

def orthogonalize_one(direction):
    fro_norm = jnp.sqrt(jnp.sum(direction * direction))
    current = (direction / (fro_norm + norm_eps)).astype(jnp.bfloat16)
    result = current.astype(jnp.float32)
    for iteration in range(ITERS):
        pieces = current.astype(jnp.float32).reshape(KV_OUT, N_NARROW, D // N_NARROW)
        partial_value = jnp.einsum('mjk,njk->jmn', pieces, pieces)
        rounded = lax.optimization_barrier(partial_value.astype(jnp.bfloat16))
        gram_sum = lax.optimization_barrier(jnp.sum(rounded.astype(jnp.float32), axis=0)).astype(jnp.bfloat16)
        square = jnp.dot(gram_sum, gram_sum, preferred_element_type=jnp.float32)
        polynomial = (coef_b * gram_sum.astype(jnp.float32) + coef_c * square).astype(jnp.bfloat16)
        result = coef_a * current.astype(jnp.float32) + jnp.dot(polynomial, current, preferred_element_type=jnp.float32)
        if iteration + 1 < ITERS:
            current = result.astype(jnp.bfloat16)
    update = (math.sqrt(D) * result).astype(jnp.bfloat16)
    mean_square = jnp.mean(update.astype(jnp.float32) * update.astype(jnp.float32))
    return (update, mean_square)

def reference(grads, momentum, owners, norm_grads, norm_params, adam_m, adam_v):
    grad_values = grads.astype(jnp.float32)
    momentum_new = muon_beta * momentum + grad_values
    direction = grad_values + muon_beta * momentum_new
    muon_update, mean_squares = lax.map(orthogonalize_one, direction)
    group_ids = jnp.arange(GROUPS, dtype=jnp.int32)
    owner_load = lax.optimization_barrier(jnp.sum(jnp.where(owners[None, :] == group_ids[:, None], mean_squares[None, :], 0.0), axis=1))
    adam_m_new = adam_first * adam_m + (1.0 - adam_first) * norm_grads
    adam_v_new = adam_second * adam_v + (1.0 - adam_second) * norm_grads * norm_grads
    corrected = adam_m_new / first_fix / (jnp.sqrt(adam_v_new / second_fix) + adam_eps)
    norm_params_new = norm_params - adam_rate * corrected
    return (muon_update, momentum_new, owner_load, norm_params_new, adam_m_new, adam_v_new)
```

```python
import functools
import math

import jax
import jax.numpy as jnp
from jax import lax
from jax.experimental import pallas as pl
from jax.experimental.pallas import tpu as pltpu
from jax.sharding import PartitionSpec as P

D = 2048
KV_OUT = 512

coef_a = 3.4445
coef_b = -4.775
coef_c = 2.0315
muon_beta = 0.95
norm_eps = 1e-07
adam_first = 0.9
adam_second = 0.95
adam_rate = 0.02
adam_eps = 1e-08
first_fix = 1.0 - 0.9**10
second_fix = 1.0 - 0.95**10

MESH = pl.DeviceIdType.MESH
BF16 = jnp.bfloat16
F32 = jnp.float32


def mul(left, right):
    return jnp.dot(left, right, preferred_element_type=F32)


def kernel(
    groups, parts, mats, chunks,
    owners, grads, momentum,
    update, momentum_new, owner_load,
    dirs, blocks, results, grams, traces, halves, load_tile, loads, fresh, ident,
    dir_send, dir_recv, res_send, res_recv, gram_send, gram_recv,
    trace_send, trace_recv, half_send, half_recv, load_send, load_recv, own_sem, mom_sem,
):
    me = lax.axis_index("wide")
    part = lax.axis_index("narrow")
    rows, cols = dirs.shape[1], dirs.shape[2]

    def matrix_of(group):
        matrix = lax.div(group * mats + (groups - 1), groups)
        owned = (lax.div(matrix * groups, mats) == group) & (matrix < mats)
        return jnp.minimum(matrix, mats - 1), owned

    my_matrix, is_owner = matrix_of(me)

    def group_at(step):
        return lax.rem(me + step, groups)

    barrier = pltpu.get_barrier_semaphore()

    @pl.loop(1, groups)
    def _(step):
        pl.semaphore_signal(barrier, inc=1, device_id=(group_at(step), part), device_id_type=MESH)

    for step in range(1, parts):
        peer = lax.rem(part + step, parts)
        pl.semaphore_signal(barrier, inc=1, device_id=(me, peer), device_id_type=MESH)

    @pl.loop(0, mats)
    def _(matrix):
        grad_values = grads[matrix].astype(F32)
        new = muon_beta * momentum[matrix] + grad_values
        fresh[matrix] = new
        dirs[matrix] = (grad_values + muon_beta * new).astype(BF16)

    pl.semaphore_wait(barrier, groups - 1 + parts - 1)

    def dir_copy(matrix, group, slot):
        return pltpu.make_async_remote_copy(
            src_ref=dirs.at[matrix], dst_ref=blocks.at[slot],
            send_sem=dir_send.at[matrix], recv_sem=dir_recv.at[slot],
            device_id=(group, part), device_id_type=MESH,
        )

    @pl.loop(0, groups)
    def _(step):
        group = group_at(step + groups // 2)
        matrix, owned = matrix_of(group)

        @pl.when(owned & (group != me))
        def _():
            dir_copy(matrix, group, me).start()

    mom_copy = pltpu.make_async_copy(fresh, momentum_new, mom_sem)
    mom_copy.start()

    def result_copy(group, matrix):
        return pltpu.make_async_remote_copy(
            src_ref=results.at[group], dst_ref=update.at[matrix],
            send_sem=res_send.at[group], recv_sem=res_recv.at[matrix],
            device_id=(group, part), device_id_type=MESH,
        )

    def load_copy(group, matrix):
        return pltpu.make_async_remote_copy(
            src_ref=load_tile, dst_ref=loads.at[matrix],
            send_sem=load_send.at[group], recv_sem=load_recv.at[matrix],
            device_id=(group, part), device_id_type=MESH,
        )

    def peer_copy(buffer, peer, slot, send, recv):
        return pltpu.make_async_remote_copy(
            src_ref=buffer.at[slot], dst_ref=buffer.at[slot],
            send_sem=send.at[peer], recv_sem=recv.at[slot],
            device_id=(me, peer), device_id_type=MESH,
        )

    @pl.when(is_owner)
    def _():
        blocks[me] = dirs[my_matrix]
        row_ids = lax.broadcasted_iota(jnp.int32, (KV_OUT, KV_OUT), 0)
        col_ids = lax.broadcasted_iota(jnp.int32, (KV_OUT, KV_OUT), 1)

        @pl.loop(1, groups)
        def _(step):
            source = group_at(step)
            dir_copy(my_matrix, me, source).wait_recv()

        matrix = blocks[...].reshape(KV_OUT, cols)
        partial_value = lax.dot_general(
            matrix, matrix, (((1,), (1,)), ((), ())), preferred_element_type=F32
        )
        grams[part] = partial_value.astype(BF16)
        squares = jnp.sum(jnp.where(row_ids == col_ids, partial_value, 0.0))
        traces[part] = jnp.full((8, 128), squares, F32)
        for step in range(1, parts):
            peer = lax.rem(part + step, parts)
            peer_copy(grams, peer, part, gram_send, gram_recv).start()
            peer_copy(traces, peer, part, trace_send, trace_recv).start()
        for step in range(1, parts):
            peer = lax.rem(part + step, parts)
            peer_copy(grams, peer, peer, gram_send, gram_recv).wait_recv()
            peer_copy(traces, peer, peer, trace_send, trace_recv).wait_recv()
        gram_sum = jnp.sum(grams[...].astype(F32), axis=0)
        square_sum = jnp.sum(traces[...], axis=0)[0:1, 0:1]
        scale = 1.0 / (jnp.sqrt(square_sum) + norm_eps)
        gram = (gram_sum * scale * scale).astype(BF16)
        gram_wide = gram.astype(F32)
        poly = coef_b * gram_wide + coef_c * mul(gram, gram)
        poly_first = poly.astype(BF16)
        mixed = mul(poly_first, gram)
        next_gram = (
            (coef_a * coef_a) * gram_wide
            + (2.0 * coef_a) * mixed
            + mul(mixed.astype(BF16), poly_first)
        ).astype(BF16)
        poly_second = (
            coef_b * next_gram.astype(F32) + coef_c * mul(next_gram, next_gram)
        )
        total = (
            coef_a * (poly_first.astype(F32) + poly_second)
            + mul(poly_second.astype(BF16), poly_first)
        )
        ident[...] = total.astype(BF16).reshape(ident.shape)

        out_scale = scale * math.sqrt(D)
        per_chunk = groups // chunks
        chunk_rows = KV_OUT // chunks
        my_chunk = lax.div(me, per_chunk)

        def chunk_body(step, square_total):
            chunk = lax.rem(my_chunk + step + chunks // 2, chunks)
            first = chunk * per_chunk
            mine = blocks[pl.ds(first, per_chunk)].reshape(chunk_rows, cols)
            factor = ident[pl.ds(first, per_chunk)].reshape(chunk_rows, KV_OUT)
            values = (coef_a * coef_a) * mine.astype(F32) + mul(
                factor, blocks[...].reshape(KV_OUT, cols)
            )
            rounded = (out_scale * values).astype(BF16)
            results[pl.ds(first, per_chunk)] = rounded.reshape(per_chunk, rows, cols)

            @pl.loop(0, per_chunk)
            def _(member):
                group = first + lax.rem(me + member, per_chunk)

                @pl.when(group != me)
                def _():
                    result_copy(group, my_matrix).start()

                @pl.when(group == me)
                def _():
                    pltpu.make_async_copy(results.at[me], update.at[my_matrix], own_sem).start()

            wide = rounded.astype(F32)
            return square_total + jnp.sum(wide * wide)

        square_total = lax.fori_loop(0, chunks, chunk_body, jnp.zeros((), F32))
        halves[part] = jnp.full((8, 128), square_total, F32)
        for step in range(1, parts):
            peer = lax.rem(part + step, parts)
            peer_copy(halves, peer, part, half_send, half_recv).start()
        for step in range(1, parts):
            peer = lax.rem(part + step, parts)
            peer_copy(halves, peer, peer, half_send, half_recv).wait_recv()
        load_tile[...] = jnp.sum(halves[...], axis=0) / (KV_OUT * D)
        loads[my_matrix] = load_tile[...]

        @pl.loop(1, groups)
        def _(step):
            load_copy(group_at(step), my_matrix).start()

        for step in range(1, parts):
            peer = lax.rem(part + step, parts)
            peer_copy(grams, peer, part, gram_send, gram_recv).wait_send()
            peer_copy(traces, peer, part, trace_send, trace_recv).wait_send()
            peer_copy(halves, peer, part, half_send, half_recv).wait_send()

        @pl.loop(1, groups)
        def _(step):
            group = group_at(step)
            result_copy(group, my_matrix).wait_send()
            load_copy(group, my_matrix).wait_send()

        pltpu.make_async_copy(results.at[me], update.at[my_matrix], own_sem).wait()

    @pl.loop(1, groups)
    def _(step):
        group = group_at(step)
        matrix, owned = matrix_of(group)

        @pl.when(owned)
        def _():
            dir_copy(matrix, group, me).wait_send()
            result_copy(me, matrix).wait_recv()
            load_copy(me, matrix).wait_recv()

    total_load = jnp.zeros((8, 128), F32)
    for matrix in range(mats):
        total_load = total_load + jnp.where(owners[matrix] == me, 1.0, 0.0) * loads[matrix]
    owner_load[...] = total_load
    mom_copy.wait()


def on_device(groups, parts, grads, momentum, owners, norm_grads, norm_params, adam_m, adam_v):
    mats, rows, cols = grads.shape
    dma = pltpu.SemaphoreType.DMA
    vmem = pl.BlockSpec(memory_space=pltpu.VMEM)
    hbm = pl.BlockSpec(memory_space=pl.ANY)
    update, momentum_new, load_block = pl.pallas_call(
        functools.partial(kernel, groups, parts, mats, 4),
        out_shape=(
            jax.ShapeDtypeStruct((mats, rows, cols), BF16),
            jax.ShapeDtypeStruct((mats, rows, cols), F32),
            jax.ShapeDtypeStruct((8, 128), F32),
        ),
        in_specs=[pl.BlockSpec(memory_space=pltpu.SMEM), vmem, vmem],
        out_specs=(hbm, hbm, vmem),
        scratch_shapes=[
            pltpu.VMEM((mats, rows, cols), BF16),
            pltpu.VMEM((groups, rows, cols), BF16),
            pltpu.VMEM((groups, rows, cols), BF16),
            pltpu.VMEM((parts, KV_OUT, KV_OUT), BF16),
            pltpu.VMEM((parts, 8, 128), F32),
            pltpu.VMEM((parts, 8, 128), F32),
            pltpu.VMEM((8, 128), F32),
            pltpu.VMEM((mats, 8, 128), F32),
            pltpu.VMEM((mats, rows, cols), F32),
            pltpu.VMEM((groups, rows, KV_OUT), BF16),
            dma((mats,)), dma((groups,)), dma((groups,)), dma((mats,)),
            dma((parts,)), dma((parts,)), dma((parts,)), dma((parts,)),
            dma((parts,)), dma((parts,)), dma((groups,)), dma((mats,)),
            dma, dma,
        ],
        compiler_params=pltpu.CompilerParams(
            collective_id=0, has_side_effects=True, vmem_limit_bytes=48 * 1024 * 1024
        ),
    )(owners, grads, momentum)
    adam_m_new = adam_first * adam_m + (1.0 - adam_first) * norm_grads
    adam_v_new = adam_second * adam_v + (1.0 - adam_second) * norm_grads * norm_grads
    corrected = adam_m_new / first_fix / (jnp.sqrt(adam_v_new / second_fix) + adam_eps)
    norm_params_new = norm_params - adam_rate * corrected
    return (update, momentum_new, load_block[0, 0:1], norm_params_new, adam_m_new, adam_v_new)


def solution(mesh):
    return jax.shard_map(
        functools.partial(on_device, mesh.shape["wide"], mesh.shape["narrow"]),
        mesh=mesh,
        in_specs=(
            P(None, "wide", "narrow"),
            P(None, "wide", "narrow"),
            P(),
            P("narrow", "wide"),
            P("narrow", "wide"),
            P("narrow", "wide"),
            P("narrow", "wide"),
        ),
        out_specs=(
            P(None, "wide", "narrow"),
            P(None, "wide", "narrow"),
            P("wide"),
            P("narrow", "wide"),
            P("narrow", "wide"),
            P("narrow", "wide"),
        ),
        check_vma=False,
    )
```

```python
import functools
import math

import jax
import jax.numpy as jnp
from jax import lax
from jax.experimental import pallas as pl
from jax.experimental.pallas import tpu as pltpu
from jax.sharding import PartitionSpec as P

D = 2048
KV_OUT = 512

coef_a = 3.4445
coef_b = -4.775
coef_c = 2.0315
muon_beta = 0.95
norm_eps = 1e-07
adam_first = 0.9
adam_second = 0.95
adam_rate = 0.02
adam_eps = 1e-08
first_fix = 1.0 - 0.9**10
second_fix = 1.0 - 0.95**10

MESH = pl.DeviceIdType.MESH
BF16 = jnp.bfloat16
F32 = jnp.float32


def mul(left, right):
    return jnp.dot(left, right, preferred_element_type=F32)


def kernel(
    groups, parts, mats, chunks,
    owners_hbm, grads_hbm, momentum_hbm,
    update, momentum_new, owner_load,
    dirs, blocks, results, grams, traces, halves, load_tile, loads, fresh, ident,
    dir_send, dir_recv, res_send, res_recv, gram_send, gram_recv,
    trace_send, trace_recv, half_send, half_recv, load_send, load_recv, own_sem, mom_sem,
    owners, grads, momentum, owners_sem, grads_sem, momentum_sem,
):
    me = lax.axis_index("wide")
    part = lax.axis_index("narrow")
    rows, cols = dirs.shape[1], dirs.shape[2]

    def matrix_of(group):
        matrix = lax.div(group * mats + (groups - 1), groups)
        owned = (lax.div(matrix * groups, mats) == group) & (matrix < mats)
        return jnp.minimum(matrix, mats - 1), owned

    my_matrix, is_owner = matrix_of(me)

    def group_at(step):
        return lax.rem(me + step, groups)

    def loads_of(matrix):
        return (
            pltpu.make_async_copy(grads_hbm.at[matrix], grads.at[matrix], grads_sem.at[matrix]),
            pltpu.make_async_copy(
                momentum_hbm.at[matrix], momentum.at[matrix], momentum_sem.at[matrix]
            ),
        )

    half = groups // 2

    def member_of(wave, step):
        place = lax.rem(me + step + half // 2, half)
        if wave == 0:
            return place + jnp.where(place < half // 2, 0, half)
        return place + half // 2

    def on_member(wave, step, body):
        group = member_of(wave, step)
        matrix, owned = matrix_of(group)

        @pl.when(owned)
        def _():
            body(matrix, group)

    def each_owner(wave, body):
        @pl.loop(0, half)
        def _(step):
            on_member(wave, step, body)

    def fetch(matrix, group):
        for copy in loads_of(matrix):
            copy.start()

    owners_copy = pltpu.make_async_copy(owners_hbm, owners, owners_sem)
    owners_copy.start()
    barrier = pltpu.get_barrier_semaphore()

    @pl.loop(1, groups)
    def _(step):
        pl.semaphore_signal(barrier, inc=1, device_id=(group_at(step), part), device_id_type=MESH)

    for step in range(1, parts):
        peer = lax.rem(part + step, parts)
        pl.semaphore_signal(barrier, inc=1, device_id=(me, peer), device_id_type=MESH)

    each_owner(0, fetch)
    each_owner(1, fetch)
    pl.semaphore_wait(barrier, groups - 1 + parts - 1)

    def dir_copy(matrix, group, slot):
        return pltpu.make_async_remote_copy(
            src_ref=dirs.at[matrix], dst_ref=blocks.at[slot],
            send_sem=dir_send.at[matrix], recv_sem=dir_recv.at[slot],
            device_id=(group, part), device_id_type=MESH,
        )

    def direct(matrix, group):
        for copy in loads_of(matrix):
            copy.wait()
        grad_values = grads[matrix].astype(F32)
        new = muon_beta * momentum[matrix] + grad_values
        fresh[matrix] = new
        dirs[matrix] = (grad_values + muon_beta * new).astype(BF16)

    def direct_and_send(matrix, group):
        direct(matrix, group)

        @pl.when(group != me)
        def _():
            dir_copy(matrix, group, me).start()

    def drain(matrix, group):
        @pl.when(group != me)
        def _():
            dir_copy(matrix, group, me).wait_send()

    def send(matrix, group):
        @pl.when(group != me)
        def _():
            dir_copy(matrix, group, me).start()

    each_owner(0, direct_and_send)
    each_owner(1, direct)
    @pl.loop(0, half // 2)
    def _(step):
        on_member(1, step, send)

    @pl.loop(0, half // 2)
    def _(step):
        on_member(0, step, drain)
        on_member(1, step + half // 2, send)

    @pl.loop(half // 2, half)
    def _(step):
        on_member(0, step, drain)


    mom_copy = pltpu.make_async_copy(fresh, momentum_new, mom_sem)
    mom_copy.start()

    def result_copy(group, matrix):
        return pltpu.make_async_remote_copy(
            src_ref=results.at[group], dst_ref=update.at[matrix],
            send_sem=res_send.at[group], recv_sem=res_recv.at[matrix],
            device_id=(group, part), device_id_type=MESH,
        )

    def load_copy(group, matrix):
        return pltpu.make_async_remote_copy(
            src_ref=load_tile, dst_ref=loads.at[matrix],
            send_sem=load_send.at[group], recv_sem=load_recv.at[matrix],
            device_id=(group, part), device_id_type=MESH,
        )

    def peer_copy(buffer, peer, slot, send, recv):
        return pltpu.make_async_remote_copy(
            src_ref=buffer.at[slot], dst_ref=buffer.at[slot],
            send_sem=send.at[peer], recv_sem=recv.at[slot],
            device_id=(me, peer), device_id_type=MESH,
        )

    @pl.when(is_owner)
    def _():
        blocks[me] = dirs[my_matrix]
        row_ids = lax.broadcasted_iota(jnp.int32, (KV_OUT, KV_OUT), 0)
        col_ids = lax.broadcasted_iota(jnp.int32, (KV_OUT, KV_OUT), 1)

        @pl.loop(1, groups)
        def _(step):
            source = group_at(step)
            dir_copy(my_matrix, me, source).wait_recv()

        matrix = blocks[...].reshape(KV_OUT, cols)
        partial_value = lax.dot_general(
            matrix, matrix, (((1,), (1,)), ((), ())), preferred_element_type=F32
        )
        grams[part] = partial_value.astype(BF16)
        squares = jnp.sum(jnp.where(row_ids == col_ids, partial_value, 0.0))
        traces[part] = jnp.full((8, 128), squares, F32)
        for step in range(1, parts):
            peer = lax.rem(part + step, parts)
            peer_copy(grams, peer, part, gram_send, gram_recv).start()
            peer_copy(traces, peer, part, trace_send, trace_recv).start()
        for step in range(1, parts):
            peer = lax.rem(part + step, parts)
            peer_copy(grams, peer, peer, gram_send, gram_recv).wait_recv()
            peer_copy(traces, peer, peer, trace_send, trace_recv).wait_recv()
        gram_sum = jnp.sum(grams[...].astype(F32), axis=0)
        square_sum = jnp.sum(traces[...], axis=0)[0:1, 0:1]
        scale = 1.0 / (jnp.sqrt(square_sum) + norm_eps)
        gram = (gram_sum * scale * scale).astype(BF16)
        gram_wide = gram.astype(F32)
        poly = coef_b * gram_wide + coef_c * mul(gram, gram)
        poly_first = poly.astype(BF16)
        mixed = mul(poly_first, gram)
        next_gram = (
            (coef_a * coef_a) * gram_wide
            + (2.0 * coef_a) * mixed
            + mul(mixed.astype(BF16), poly_first)
        ).astype(BF16)
        poly_second = (
            coef_b * next_gram.astype(F32) + coef_c * mul(next_gram, next_gram)
        )
        total = (
            coef_a * (poly_first.astype(F32) + poly_second)
            + mul(poly_second.astype(BF16), poly_first)
        )
        ident[...] = total.astype(BF16).reshape(ident.shape)

        out_scale = scale * math.sqrt(D)
        per_chunk = groups // chunks
        chunk_rows = KV_OUT // chunks
        my_chunk = lax.div(me, per_chunk)

        def chunk_body(step, square_total):
            chunk = lax.rem(my_chunk + step + chunks // 2, chunks)
            first = chunk * per_chunk
            mine = blocks[pl.ds(first, per_chunk)].reshape(chunk_rows, cols)
            factor = ident[pl.ds(first, per_chunk)].reshape(chunk_rows, KV_OUT)
            values = (coef_a * coef_a) * mine.astype(F32) + mul(
                factor, blocks[...].reshape(KV_OUT, cols)
            )
            rounded = (out_scale * values).astype(BF16)
            results[pl.ds(first, per_chunk)] = rounded.reshape(per_chunk, rows, cols)

            @pl.loop(0, per_chunk)
            def _(member):
                group = first + lax.rem(me + member, per_chunk)

                @pl.when(group != me)
                def _():
                    result_copy(group, my_matrix).start()

                @pl.when(group == me)
                def _():
                    pltpu.make_async_copy(results.at[me], update.at[my_matrix], own_sem).start()

            wide = rounded.astype(F32)
            return square_total + jnp.sum(wide * wide)

        square_total = lax.fori_loop(0, chunks, chunk_body, jnp.zeros((), F32))
        halves[part] = jnp.full((8, 128), square_total, F32)
        for step in range(1, parts):
            peer = lax.rem(part + step, parts)
            peer_copy(halves, peer, part, half_send, half_recv).start()
        for step in range(1, parts):
            peer = lax.rem(part + step, parts)
            peer_copy(halves, peer, peer, half_send, half_recv).wait_recv()
        load_tile[...] = jnp.sum(halves[...], axis=0) / (KV_OUT * D)
        loads[my_matrix] = load_tile[...]

        @pl.loop(1, groups)
        def _(step):
            load_copy(group_at(step), my_matrix).start()

        for step in range(1, parts):
            peer = lax.rem(part + step, parts)
            peer_copy(grams, peer, part, gram_send, gram_recv).wait_send()
            peer_copy(traces, peer, part, trace_send, trace_recv).wait_send()
            peer_copy(halves, peer, part, half_send, half_recv).wait_send()

        @pl.loop(1, groups)
        def _(step):
            group = group_at(step)
            result_copy(group, my_matrix).wait_send()
            load_copy(group, my_matrix).wait_send()

        pltpu.make_async_copy(results.at[me], update.at[my_matrix], own_sem).wait()

    each_owner(1, drain)

    @pl.loop(1, groups)
    def _(step):
        group = group_at(step)
        matrix, owned = matrix_of(group)

        @pl.when(owned)
        def _():
            result_copy(me, matrix).wait_recv()
            load_copy(me, matrix).wait_recv()

    owners_copy.wait()
    total_load = jnp.zeros((8, 128), F32)
    for matrix in range(mats):
        total_load = total_load + jnp.where(owners[matrix] == me, 1.0, 0.0) * loads[matrix]
    owner_load[...] = total_load
    mom_copy.wait()


def on_device(groups, parts, grads, momentum, owners, norm_grads, norm_params, adam_m, adam_v):
    mats, rows, cols = grads.shape
    dma = pltpu.SemaphoreType.DMA
    vmem = pl.BlockSpec(memory_space=pltpu.VMEM)
    hbm = pl.BlockSpec(memory_space=pl.ANY)
    update, momentum_new, load_block = pl.pallas_call(
        functools.partial(kernel, groups, parts, mats, 4),
        out_shape=(
            jax.ShapeDtypeStruct((mats, rows, cols), BF16),
            jax.ShapeDtypeStruct((mats, rows, cols), F32),
            jax.ShapeDtypeStruct((8, 128), F32),
        ),
        in_specs=[pl.BlockSpec(memory_space=pltpu.HBM)] * 3,
        out_specs=(hbm, hbm, vmem),
        scratch_shapes=[
            pltpu.VMEM((mats, rows, cols), BF16),
            pltpu.VMEM((groups, rows, cols), BF16),
            pltpu.VMEM((groups, rows, cols), BF16),
            pltpu.VMEM((parts, KV_OUT, KV_OUT), BF16),
            pltpu.VMEM((parts, 8, 128), F32),
            pltpu.VMEM((parts, 8, 128), F32),
            pltpu.VMEM((8, 128), F32),
            pltpu.VMEM((mats, 8, 128), F32),
            pltpu.VMEM((mats, rows, cols), F32),
            pltpu.VMEM((groups, rows, KV_OUT), BF16),
            dma((mats,)), dma((groups,)), dma((groups,)), dma((mats,)),
            dma((parts,)), dma((parts,)), dma((parts,)), dma((parts,)),
            dma((parts,)), dma((parts,)), dma((groups,)), dma((mats,)),
            dma, dma,
            pltpu.SMEM((mats,), jnp.int32),
            pltpu.VMEM((mats, rows, cols), BF16),
            pltpu.VMEM((mats, rows, cols), F32),
            dma, dma((mats,)), dma((mats,)),
        ],
        compiler_params=pltpu.CompilerParams(
            collective_id=0, has_side_effects=True, vmem_limit_bytes=60 * 1024 * 1024
        ),
    )(owners, grads, momentum)
    adam_m_new = adam_first * adam_m + (1.0 - adam_first) * norm_grads
    adam_v_new = adam_second * adam_v + (1.0 - adam_second) * norm_grads * norm_grads
    corrected = adam_m_new / first_fix / (jnp.sqrt(adam_v_new / second_fix) + adam_eps)
    norm_params_new = norm_params - adam_rate * corrected
    return (update, momentum_new, load_block[0, 0:1], norm_params_new, adam_m_new, adam_v_new)


def solution(mesh):
    return jax.shard_map(
        functools.partial(on_device, mesh.shape["wide"], mesh.shape["narrow"]),
        mesh=mesh,
        in_specs=(
            P(None, "wide", "narrow"),
            P(None, "wide", "narrow"),
            P(),
            P("narrow", "wide"),
            P("narrow", "wide"),
            P("narrow", "wide"),
            P("narrow", "wide"),
        ),
        out_specs=(
            P(None, "wide", "narrow"),
            P(None, "wide", "narrow"),
            P("wide"),
            P("narrow", "wide"),
            P("narrow", "wide"),
            P("narrow", "wide"),
        ),
        check_vma=False,
    )
```

```python
import functools
import math

import jax
import jax.numpy as jnp
from jax import lax
from jax.experimental import pallas as pl
from jax.experimental.pallas import tpu as pltpu
from jax.sharding import PartitionSpec as P

D = 2048
KV_OUT = 512

coef_a = 3.4445
coef_b = -4.775
coef_c = 2.0315
muon_beta = 0.95
norm_eps = 1e-07
adam_first = 0.9
adam_second = 0.95
adam_rate = 0.02
adam_eps = 1e-08
first_fix = 1.0 - 0.9**10
second_fix = 1.0 - 0.95**10

MESH = pl.DeviceIdType.MESH
BF16 = jnp.bfloat16
F32 = jnp.float32


def mul(left, right):
    return jnp.dot(left, right, preferred_element_type=F32)


def kernel(
    groups, parts, mats, chunks,
    owners_hbm, grads_hbm, momentum_hbm,
    update, momentum_new, owner_load,
    dirs, blocks, results, grams, traces, halves, load_tile, loads, fresh, ident,
    dir_send, dir_recv, res_send, res_recv, gram_send, gram_recv,
    trace_send, trace_recv, half_send, half_recv, load_send, load_recv, own_sem, mom_sem,
    owners, grads, momentum, owners_sem, grads_sem, momentum_sem,
):
    me = lax.axis_index("wide")
    part = lax.axis_index("narrow")
    rows, cols = dirs.shape[1], dirs.shape[2]

    def matrix_of(group):
        matrix = lax.div(group * mats + (groups - 1), groups)
        owned = (lax.div(matrix * groups, mats) == group) & (matrix < mats)
        return jnp.minimum(matrix, mats - 1), owned

    my_matrix, is_owner = matrix_of(me)

    def group_at(step):
        return lax.rem(me + step, groups)

    def loads_of(matrix):
        return (
            pltpu.make_async_copy(grads_hbm.at[matrix], grads.at[matrix], grads_sem.at[matrix]),
            pltpu.make_async_copy(
                momentum_hbm.at[matrix], momentum.at[matrix], momentum_sem.at[matrix]
            ),
        )

    half = groups // 2

    def member_of(wave, step):
        place = lax.rem(me + step + half // 2, half)
        if wave == 0:
            return place + jnp.where(place < half // 2, 0, half)
        return place + half // 2

    def on_member(wave, step, body):
        group = member_of(wave, step)
        matrix, owned = matrix_of(group)

        @pl.when(owned)
        def _():
            body(matrix, group)

    def each_owner(wave, body):
        @pl.loop(0, half)
        def _(step):
            on_member(wave, step, body)

    def fetch(matrix, group):
        for copy in loads_of(matrix):
            copy.start()

    owners_copy = pltpu.make_async_copy(owners_hbm, owners, owners_sem)
    owners_copy.start()
    barrier = pltpu.get_barrier_semaphore()

    @pl.loop(1, groups)
    def _(step):
        pl.semaphore_signal(barrier, inc=1, device_id=(group_at(step), part), device_id_type=MESH)

    for step in range(1, parts):
        peer = lax.rem(part + step, parts)
        pl.semaphore_signal(barrier, inc=1, device_id=(me, peer), device_id_type=MESH)

    each_owner(0, fetch)
    each_owner(1, fetch)
    pl.semaphore_wait(barrier, groups - 1 + parts - 1)

    def dir_copy(matrix, group, slot):
        return pltpu.make_async_remote_copy(
            src_ref=dirs.at[matrix], dst_ref=blocks.at[slot],
            send_sem=dir_send.at[matrix], recv_sem=dir_recv.at[slot],
            device_id=(group, part), device_id_type=MESH,
        )

    def direct(matrix, group):
        for copy in loads_of(matrix):
            copy.wait()
        grad_values = grads[matrix].astype(F32)
        new = muon_beta * momentum[matrix] + grad_values
        fresh[matrix] = new
        dirs[matrix] = (grad_values + muon_beta * new).astype(BF16)

    def direct_and_send(matrix, group):
        direct(matrix, group)

        @pl.when(group != me)
        def _():
            dir_copy(matrix, group, me).start()

    def drain(matrix, group):
        @pl.when(group != me)
        def _():
            dir_copy(matrix, group, me).wait_send()

    def send(matrix, group):
        @pl.when(group != me)
        def _():
            dir_copy(matrix, group, me).start()

    each_owner(0, direct_and_send)
    each_owner(1, direct)
    @pl.loop(0, half // 2)
    def _(step):
        on_member(1, step, send)

    @pl.loop(0, half // 2)
    def _(step):
        on_member(0, step, drain)
        on_member(1, step + half // 2, send)

    @pl.loop(half // 2, half)
    def _(step):
        on_member(0, step, drain)


    mom_copy = pltpu.make_async_copy(fresh, momentum_new, mom_sem)
    mom_copy.start()

    def result_copy(group, matrix):
        return pltpu.make_async_remote_copy(
            src_ref=results.at[group], dst_ref=update.at[matrix],
            send_sem=res_send.at[group], recv_sem=res_recv.at[matrix],
            device_id=(group, part), device_id_type=MESH,
        )

    def load_copy(group, matrix):
        return pltpu.make_async_remote_copy(
            src_ref=load_tile, dst_ref=loads.at[matrix],
            send_sem=load_send.at[group], recv_sem=load_recv.at[matrix],
            device_id=(group, part), device_id_type=MESH,
        )

    def peer_copy(buffer, peer, slot, send, recv):
        return pltpu.make_async_remote_copy(
            src_ref=buffer.at[slot], dst_ref=buffer.at[slot],
            send_sem=send.at[peer], recv_sem=recv.at[slot],
            device_id=(me, peer), device_id_type=MESH,
        )

    @pl.when(is_owner)
    def _():
        blocks[me] = dirs[my_matrix]
        row_ids = lax.broadcasted_iota(jnp.int32, (KV_OUT, KV_OUT), 0)
        col_ids = lax.broadcasted_iota(jnp.int32, (KV_OUT, KV_OUT), 1)

        @pl.loop(1, groups)
        def _(step):
            source = group_at(step)
            dir_copy(my_matrix, me, source).wait_recv()

        matrix = blocks[...].reshape(KV_OUT, cols)
        partial_value = lax.dot_general(
            matrix, matrix, (((1,), (1,)), ((), ())), preferred_element_type=F32
        )
        grams[part] = partial_value.astype(BF16)
        squares = jnp.sum(jnp.where(row_ids == col_ids, partial_value, 0.0))
        traces[part] = jnp.full((8, 128), squares, F32)
        for step in range(1, parts):
            peer = lax.rem(part + step, parts)
            peer_copy(grams, peer, part, gram_send, gram_recv).start()
            peer_copy(traces, peer, part, trace_send, trace_recv).start()
        for step in range(1, parts):
            peer = lax.rem(part + step, parts)
            peer_copy(grams, peer, peer, gram_send, gram_recv).wait_recv()
            peer_copy(traces, peer, peer, trace_send, trace_recv).wait_recv()
        gram_sum = jnp.sum(grams[...].astype(F32), axis=0)
        square_sum = jnp.sum(traces[...], axis=0)[0:1, 0:1]
        scale = 1.0 / (jnp.sqrt(square_sum) + norm_eps)
        gram = (gram_sum * scale * scale).astype(BF16)
        gram_wide = gram.astype(F32)
        poly = coef_b * gram_wide + coef_c * mul(gram, gram)
        poly_first = poly.astype(BF16)
        mixed = mul(poly_first, gram)
        next_gram = (
            (coef_a * coef_a) * gram_wide
            + (2.0 * coef_a) * mixed
            + mul(mixed.astype(BF16), poly_first)
        ).astype(BF16)
        poly_second = (
            coef_b * next_gram.astype(F32) + coef_c * mul(next_gram, next_gram)
        )
        total = (
            coef_a * (poly_first.astype(F32) + poly_second)
            + mul(poly_second.astype(BF16), poly_first)
        )
        ident[...] = total.astype(BF16).reshape(ident.shape)

        out_scale = scale * math.sqrt(D)
        per_chunk = groups // chunks
        chunk_rows = KV_OUT // chunks
        my_chunk = lax.div(me, per_chunk)

        def chunk_body(step, square_total):
            chunk = lax.rem(my_chunk + step + chunks // 2, chunks)
            first = chunk * per_chunk
            mine = blocks[pl.ds(first, per_chunk)].reshape(chunk_rows, cols)
            factor = ident[pl.ds(first, per_chunk)].reshape(chunk_rows, KV_OUT)
            values = (coef_a * coef_a) * mine.astype(F32) + mul(
                factor, blocks[...].reshape(KV_OUT, cols)
            )
            rounded = (out_scale * values).astype(BF16)
            results[pl.ds(first, per_chunk)] = rounded.reshape(per_chunk, rows, cols)

            @pl.loop(0, per_chunk)
            def _(member):
                group = first + lax.rem(me + member, per_chunk)

                @pl.when(group != me)
                def _():
                    result_copy(group, my_matrix).start()

                @pl.when(group == me)
                def _():
                    pltpu.make_async_copy(results.at[me], update.at[my_matrix], own_sem).start()

            wide = rounded.astype(F32)
            return square_total + jnp.sum(wide * wide)

        square_total = lax.fori_loop(0, chunks, chunk_body, jnp.zeros((), F32))
        halves[part] = jnp.full((8, 128), square_total, F32)
        for step in range(1, parts):
            peer = lax.rem(part + step, parts)
            peer_copy(halves, peer, part, half_send, half_recv).start()
        for step in range(1, parts):
            peer = lax.rem(part + step, parts)
            peer_copy(halves, peer, peer, half_send, half_recv).wait_recv()
        load_tile[...] = jnp.sum(halves[...], axis=0) / (KV_OUT * D)
        loads[my_matrix] = load_tile[...]

        @pl.loop(1, groups)
        def _(step):
            load_copy(group_at(step), my_matrix).start()

        for step in range(1, parts):
            peer = lax.rem(part + step, parts)
            peer_copy(grams, peer, part, gram_send, gram_recv).wait_send()
            peer_copy(traces, peer, part, trace_send, trace_recv).wait_send()
            peer_copy(halves, peer, part, half_send, half_recv).wait_send()

        @pl.loop(1, groups)
        def _(step):
            group = group_at(step)
            result_copy(group, my_matrix).wait_send()
            load_copy(group, my_matrix).wait_send()

        pltpu.make_async_copy(results.at[me], update.at[my_matrix], own_sem).wait()

    each_owner(1, drain)

    @pl.loop(1, groups)
    def _(step):
        group = group_at(step)
        matrix, owned = matrix_of(group)

        @pl.when(owned)
        def _():
            result_copy(me, matrix).wait_recv()
            load_copy(me, matrix).wait_recv()

    owners_copy.wait()
    total_load = jnp.zeros((8, 128), F32)
    for matrix in range(mats):
        total_load = total_load + jnp.where(owners[matrix] == me, 1.0, 0.0) * loads[matrix]
    owner_load[...] = total_load
    mom_copy.wait()


def finish(
    update, momentum, load_block, norm_grads, norm_params, adam_m, adam_v,
    update_out, momentum_out, load_out, params_out, adam_m_out, adam_v_out,
    update_sem, momentum_sem,
):
    momentum_copy = pltpu.make_async_copy(momentum, momentum_out, momentum_sem)
    update_copy = pltpu.make_async_copy(update, update_out, update_sem)
    momentum_copy.start()
    update_copy.start()
    grad = norm_grads[...]
    adam_m_new = adam_first * adam_m[...] + (1.0 - adam_first) * grad
    adam_v_new = adam_second * adam_v[...] + (1.0 - adam_second) * grad * grad
    corrected = adam_m_new / first_fix / (jnp.sqrt(adam_v_new / second_fix) + adam_eps)
    params_out[...] = norm_params[...] - adam_rate * corrected
    adam_m_out[...] = adam_m_new
    adam_v_out[...] = adam_v_new
    load_out[0] = load_block[0, 0]
    momentum_copy.wait()
    update_copy.wait()


def on_device(groups, parts, grads, momentum, owners, norm_grads, norm_params, adam_m, adam_v):
    mats, rows, cols = grads.shape
    dma = pltpu.SemaphoreType.DMA
    vmem = pl.BlockSpec(memory_space=pltpu.VMEM)
    hbm = pl.BlockSpec(memory_space=pl.ANY)
    update, momentum_new, load_block = pl.pallas_call(
        functools.partial(kernel, groups, parts, mats, 4),
        out_shape=(
            jax.ShapeDtypeStruct((mats, rows, cols), BF16),
            jax.ShapeDtypeStruct((mats, rows, cols), F32),
            jax.ShapeDtypeStruct((8, 128), F32),
        ),
        in_specs=[pl.BlockSpec(memory_space=pltpu.HBM)] * 3,
        out_specs=(hbm, hbm, vmem),
        scratch_shapes=[
            pltpu.VMEM((mats, rows, cols), BF16),
            pltpu.VMEM((groups, rows, cols), BF16),
            pltpu.VMEM((groups, rows, cols), BF16),
            pltpu.VMEM((parts, KV_OUT, KV_OUT), BF16),
            pltpu.VMEM((parts, 8, 128), F32),
            pltpu.VMEM((parts, 8, 128), F32),
            pltpu.VMEM((8, 128), F32),
            pltpu.VMEM((mats, 8, 128), F32),
            pltpu.VMEM((mats, rows, cols), F32),
            pltpu.VMEM((groups, rows, KV_OUT), BF16),
            dma((mats,)), dma((groups,)), dma((groups,)), dma((mats,)),
            dma((parts,)), dma((parts,)), dma((parts,)), dma((parts,)),
            dma((parts,)), dma((parts,)), dma((groups,)), dma((mats,)),
            dma, dma,
            pltpu.SMEM((mats,), jnp.int32),
            pltpu.VMEM((mats, rows, cols), BF16),
            pltpu.VMEM((mats, rows, cols), F32),
            dma, dma((mats,)), dma((mats,)),
        ],
        compiler_params=pltpu.CompilerParams(
            collective_id=0, has_side_effects=True, vmem_limit_bytes=60 * 1024 * 1024
        ),
    )(owners, grads, momentum)
    norm_shape = jax.ShapeDtypeStruct(norm_grads.shape, F32)
    update, momentum_new, owner_load, norm_params_new, adam_m_new, adam_v_new = pl.pallas_call(
        finish,
        out_shape=(
            jax.ShapeDtypeStruct(update.shape, BF16),
            jax.ShapeDtypeStruct(momentum_new.shape, F32),
            jax.ShapeDtypeStruct((1,), F32),
            norm_shape, norm_shape, norm_shape,
        ),
        in_specs=[vmem] * 7,
        out_specs=(hbm, hbm, pl.BlockSpec(memory_space=pltpu.SMEM), vmem, vmem, vmem),
        scratch_shapes=[dma, dma],
    )(update, momentum_new, load_block, norm_grads, norm_params, adam_m, adam_v)
    return (update, momentum_new, owner_load, norm_params_new, adam_m_new, adam_v_new)


def solution(mesh):
    return jax.shard_map(
        functools.partial(on_device, mesh.shape["wide"], mesh.shape["narrow"]),
        mesh=mesh,
        in_specs=(
            P(None, "wide", "narrow"),
            P(None, "wide", "narrow"),
            P(),
            P("narrow", "wide"),
            P("narrow", "wide"),
            P("narrow", "wide"),
            P("narrow", "wide"),
        ),
        out_specs=(
            P(None, "wide", "narrow"),
            P(None, "wide", "narrow"),
            P("wide"),
            P("narrow", "wide"),
            P("narrow", "wide"),
            P("narrow", "wide"),
        ),
        check_vma=False,
    )
```
